32 devices in a mesh: ga: 8 (over y, x, core), band: 4 (over z).
Axes of the slice: x: 2, y: 2, z: 4, core: 2. Of those that a mesh axis runs over, the one named last changes fastest.
Arguments:
- psi: bfloat16 [2, 8, 96, 2048], P(None, 'band', None, 'ga'), may hold values from -6 to 6
- vloc: float32 [96, 9216], P('ga'), may hold values from 0.5 to 1.5
- dv: float32 [96, 9216], P('ga'), may hold values from -6 to 6
- beta: float32 [2, 128, 96, 2048], P(None, None, None, 'ga'), may hold values from -0.02734375 to 0.02734375
- dij: float32 [2, 4, 4], replicated, may hold values from -1 to 1.5, as said below
- atom_type: int32 [32], replicated, may hold values from 0 to 1
- stick_xy: int32 [2048], replicated, may hold values from 0 to 9215, as said below
- band_shift: float32 [8], P('band'), may hold values from 0.3 to 3
Outputs:
- response: float32 [2, 8, 96, 2048], P(None, 'band', None, 'ga')
- density: float32 [96, 9216], P('ga', 'band')
The draws below stay inside these ranges and needn't reach their ends.
Inputs may be any that keep to these rules, and one draw needn't show every extreme that they name: `stick_xy`: 2048 distinct columns, each with both frequencies f(y) and f(x) in -(32) to 31. `dij`: each of the 2 matrices is symmetric positive definite with diagonal at least 0.5.
All inputs are finite; a program needn't handle non-finite values.
Results may differ from the reference program's by a relative error of at most 0.0003.
Values may be sent and summed in bfloat16 or wider, within the bound.
A program may use at most 128 MiB of HBM per device.

```python
import math
import jax
import jax.numpy as jnp
from jax import lax

GRID = 96
STICKS = 2048
NATOM = 32
NBETA = 4
NTYPE = 2
ITERS = 2
NPROJ = 128
BANDS = 8


def draw_stick_xy(key, part):
    radius_cells = GRID // 3
    square_side = 2 * radius_cells
    chosen = jax.random.permutation(key, square_side * square_side)[:STICKS]
    freq_y = chosen // square_side - radius_cells
    freq_x = chosen % square_side - radius_cells
    return (freq_y % GRID * GRID + freq_x % GRID).astype(jnp.int32)


def draw_dij(key, part):
    factor = jax.random.uniform(key, (NTYPE, NBETA, NBETA), jnp.float32, -1.0, 1.0)
    product = jnp.einsum('tij,tkj->tik', factor, factor) / NBETA
    return product + 0.5 * jnp.eye(NBETA, dtype=jnp.float32)[None]


def with_ends(values, key, least, largest):
    dims = values.shape
    spot = [jax.random.randint(jax.random.fold_in(key, axis), (), 0, dims[axis]) for axis in range(len(dims))]
    values = values.at[tuple(spot)].set(least)
    longest = dims.index(max(dims))
    spot[longest] = (spot[longest] + 1) % dims[longest]
    return values.at[tuple(spot)].set(largest)


def level_of(key, dims, cuts, low, high):
    gain = 1.0
    for dim, parts in cuts:
        draws = jax.random.uniform(jax.random.fold_in(jax.random.fold_in(key, 6), dim), (parts,), jnp.float32, low / len(cuts), high / len(cuts))
        gain = gain * jnp.repeat(jnp.exp(draws), dims[dim] // parts).reshape((-1,) + (1,) * (len(dims) - 1 - dim))
    return gain


def noise(rng, dims, width, reach, shards=(), kind=jnp.bfloat16):
    entries = jax.random.normal(rng, dims, jnp.float32) * width
    if len(shards) > 0:
        entries = level_of(rng, dims, shards, -0.22, 0.18) * entries
    return jnp.clip(entries, min=-reach, max=reach).astype(kind)


def setup_inputs(seed: int = 0) -> dict:
    streams_of = jax.random.split(jax.random.key(seed), 9)
    return {
        "psi": noise(streams_of[0], (2, BANDS, GRID, STICKS), 1.0, 6.0, ((1, 4), (3, 8))),
        "vloc": jnp.clip(0.5 + 1.0 * jax.random.uniform(streams_of[1], (GRID, GRID * GRID), jnp.float32) ** level_of(streams_of[1], (GRID, GRID * GRID), ((0, 8),), -0.2, 0.2), 0.5, 1.5),
        "dv": noise(streams_of[2], (GRID, GRID * GRID), 1.0, 6.0, ((0, 8),), jnp.float32),
        "beta": noise(streams_of[3], (2, NPROJ, GRID, STICKS), (GRID * STICKS // 4) ** -0.5, 0.02734375, ((3, 8),), jnp.float32),
        "dij": draw_dij(jax.random.fold_in(streams_of[8], 71), 0),
        "atom_type": with_ends(jax.random.randint(streams_of[5], (NATOM,), 0, NTYPE), jax.random.fold_in(streams_of[5], 1), 0, NTYPE - 1).astype(jnp.int32),
        "stick_xy": draw_stick_xy(jax.random.fold_in(streams_of[8], 71), 0),
        "band_shift": jnp.clip(jnp.exp(math.log(3.0) - 2.3025851 * jax.random.uniform(streams_of[7], (BANDS,), jnp.float32) ** level_of(streams_of[7], (BANDS,), ((0, 4),), -0.2, 0.2)), 0.3, 3.0),
    }


highest = lax.Precision.HIGHEST


def frequency(index):
    return (index + GRID // 2) % GRID - GRID // 2


def kinetic_table(stick_xy):
    freq_z = frequency(jnp.arange(GRID, dtype=jnp.int32))
    freq_y = frequency(stick_xy // GRID)
    freq_x = frequency(stick_xy % GRID)
    summed = freq_z[:, None] ** 2 + (freq_y ** 2 + freq_x ** 2)[None, :]
    return summed.astype(jnp.float32) * (4.0 / (GRID * GRID))


def to_real(coef, stick_xy):
    values = coef[0] + 1j * coef[1]
    grid = jnp.zeros((GRID, GRID * GRID), values.dtype).at[:, stick_xy].set(values)
    field = jnp.fft.ifftn(grid.reshape(GRID, GRID, GRID)) * (GRID ** 1.5)
    field = field.reshape(GRID, GRID * GRID)
    return jnp.stack([jnp.real(field), jnp.imag(field)])


def to_recip(field, stick_xy):
    values = (field[0] + 1j * field[1]).reshape(GRID, GRID, GRID)
    spectrum = jnp.fft.fftn(values).reshape(GRID, GRID * GRID) / (GRID ** 1.5)
    picked = spectrum[:, stick_xy]
    return jnp.stack([jnp.real(picked), jnp.imag(picked)])


def reference(psi, vloc, dv, beta, dij, atom_type, stick_xy, band_shift):
    occupied = jnp.moveaxis(psi.astype(jnp.float32), 1, 0)
    kinetic = kinetic_table(stick_xy)
    inv_norm = 1.0 / (2.0 * GRID * STICKS)

    def dv_image(coef):
        return to_recip(dv[None] * to_real(coef, stick_xy), stick_xy)

    image = lax.map(dv_image, occupied)
    intersect_re = jnp.einsum('mczs,nczs->mn', occupied, image, precision=highest) * inv_norm
    intersect_im = (jnp.einsum('mzs,nzs->mn', occupied[:, 0], image[:, 1], precision=highest) - jnp.einsum('mzs,nzs->mn', occupied[:, 1], image[:, 0], precision=highest)) * inv_norm
    corr_re = jnp.einsum('mn,mzs->nzs', intersect_re, occupied[:, 0], precision=highest) - jnp.einsum('mn,mzs->nzs', intersect_im, occupied[:, 1], precision=highest)
    corr_im = jnp.einsum('mn,mzs->nzs', intersect_im, occupied[:, 0], precision=highest) + jnp.einsum('mn,mzs->nzs', intersect_re, occupied[:, 1], precision=highest)
    rhs = jnp.stack([corr_re, corr_im], axis=1) - image
    selected = dij[atom_type]
    diagonal = kinetic[None] + band_shift[:, None, None]

    def local_image(coef):
        return to_recip(vloc[None] * to_real(coef, stick_xy), stick_xy)

    def apply_operator(vector):
        local = lax.map(local_image, vector)
        proj_re = jnp.einsum('jzs,bzs->bj', beta[0], vector[:, 0], precision=highest) + jnp.einsum('jzs,bzs->bj', beta[1], vector[:, 1], precision=highest)
        proj_im = jnp.einsum('jzs,bzs->bj', beta[0], vector[:, 1], precision=highest) - jnp.einsum('jzs,bzs->bj', beta[1], vector[:, 0], precision=highest)
        shaped_re = proj_re.reshape(BANDS, NATOM, NBETA)
        shaped_im = proj_im.reshape(BANDS, NATOM, NBETA)
        coup_re = jnp.einsum('aij,baj->bai', selected, shaped_re, precision=highest).reshape(BANDS, NPROJ)
        coup_im = jnp.einsum('aij,baj->bai', selected, shaped_im, precision=highest).reshape(BANDS, NPROJ)
        back_re = jnp.einsum('jzs,bj->bzs', beta[0], coup_re, precision=highest) - jnp.einsum('jzs,bj->bzs', beta[1], coup_im, precision=highest)
        back_im = jnp.einsum('jzs,bj->bzs', beta[0], coup_im, precision=highest) + jnp.einsum('jzs,bj->bzs', beta[1], coup_re, precision=highest)
        return diagonal[:, None] * vector + local + jnp.stack([back_re, back_im], axis=1)

    def band_sum(first, second):
        return jnp.sum(first * second, axis=(1, 2, 3))

    solution = jnp.zeros_like(rhs)
    residual = rhs
    direction = rhs
    norm_now = band_sum(rhs, rhs)
    for iteration in range(ITERS):
        image_now = apply_operator(direction)
        alpha = (norm_now / band_sum(direction, image_now))[:, None, None, None]
        solution = solution + alpha * direction
        residual = residual - alpha * image_now
        if iteration + 1 < ITERS:
            norm_next = band_sum(residual, residual)
            direction = residual + (norm_next / norm_now)[:, None, None, None] * direction
            norm_now = norm_next

    def accumulate(carry, pair):
        psi_field = to_real(pair[0], stick_xy)
        resp_field = to_real(pair[1], stick_xy)
        return carry + 4.0 * jnp.sum(psi_field * resp_field, axis=0), None

    density, unused = lax.scan(accumulate, jnp.zeros((GRID, GRID * GRID), jnp.float32), (occupied, solution))
    return jnp.moveaxis(solution, 0, 1), density
```

```python
import math

import jax
import jax.numpy as jnp
import numpy as np
from jax import lax
from jax.experimental import pallas as pl
from jax.experimental.pallas import tpu as pltpu
from jax.sharding import PartitionSpec as P

LANES = 128
high = lax.Precision.HIGH


def frequency(index, grid):
    return (index + grid // 2) % grid - grid // 2


def phases(rows, cols, grid, sign):
    angle = 2.0 * math.pi * ((rows[:, None] * cols[None, :]) % grid) / grid
    factor = 1.0 / math.sqrt(grid)
    return np.cos(angle) * factor, sign * np.sin(angle) * factor


def as_f32(table):
    return jnp.asarray(table.astype(np.float32))


def packed(table):
    real, imag = table
    return np.block([[real, imag], [-imag, real]])


def pad_part(real, imag, axis):
    width = LANES - real.shape[axis]
    pads = [(0, 0), (0, 0)]
    pads[axis] = (0, width)
    return np.pad(real, pads), np.pad(imag, pads)


def hi_lo(values):
    hi = lax.reduce_precision(values, 8, 7)
    return jnp.concatenate([hi, values - hi]).astype(jnp.bfloat16)


def project_kernel(beta_ref, vec_ref, out_ref):
    bands = vec_ref.shape[1]
    lanes = vec_ref.shape[3]

    def fold(prod):
        row = jnp.sum(prod, axis=0, keepdims=True)
        total = row[:, :LANES]
        for at in range(LANES, lanes, LANES):
            total = total + row[:, at : at + LANES]
        return total

    def body(j, carry):
        b_re = beta_ref[0, j]
        b_im = beta_ref[1, j]
        rows = []
        for b in range(bands):
            v_re = vec_ref[0, b]
            v_im = vec_ref[1, b]
            rows.append(fold(b_re * v_re + b_im * v_im))
            rows.append(fold(b_re * v_im - b_im * v_re))
        out_ref[j] = jnp.concatenate(rows, axis=0)
        return carry

    lax.fori_loop(0, beta_ref.shape[1], body, 0)


def project(beta, vec):
    parts, count, grid, sticks = beta.shape
    bands = vec.shape[1]
    step = math.gcd(count, 8)
    out = pl.pallas_call(
        project_kernel,
        grid=(count // step,),
        in_specs=[
            pl.BlockSpec((parts, step, grid, sticks), lambda i: (0, i, 0, 0)),
            pl.BlockSpec(vec.shape, lambda i: (0, 0, 0, 0)),
        ],
        out_specs=pl.BlockSpec((step, 2 * bands, LANES), lambda i: (i, 0, 0)),
        out_shape=jax.ShapeDtypeStruct((count, 2 * bands, LANES), jnp.float32),
        cost_estimate=pl.CostEstimate(
            flops=4 * beta.size * bands, bytes_accessed=4 * beta.size, transcendentals=0
        ),
        name="project",
    )(beta, vec)
    return jnp.sum(out, axis=2).reshape(count, bands, 2)


def spread_kernel(coef_ref, beta_ref, out_ref):
    step = beta_ref.shape[1]
    bands = out_ref.shape[1]
    grid = out_ref.shape[2]
    base = pl.program_id(0) * step
    rows = math.gcd(grid, 16)

    @pl.when(pl.program_id(0) == 0)
    def _():
        out_ref[...] = jnp.zeros_like(out_ref)

    def body(at, carry):
        z = pl.ds(pl.multiple_of(at * rows, rows), rows)
        re = [out_ref[0, b, z, :] for b in range(bands)]
        im = [out_ref[1, b, z, :] for b in range(bands)]
        for j in range(step):
            b_re = beta_ref[0, j, z, :]
            b_im = beta_ref[1, j, z, :]
            for b in range(bands):
                c_re = coef_ref[(base + j) * 2 * bands + 2 * b]
                c_im = coef_ref[(base + j) * 2 * bands + 2 * b + 1]
                re[b] = re[b] + b_re * c_re - b_im * c_im
                im[b] = im[b] + b_re * c_im + b_im * c_re
        for b in range(bands):
            out_ref[0, b, z, :] = re[b]
            out_ref[1, b, z, :] = im[b]
        return carry

    lax.fori_loop(0, grid // rows, body, 0)


def back_project(beta, coupled):
    parts, count, grid, sticks = beta.shape
    bands = coupled.shape[1]
    step = math.gcd(count, 8)
    return pl.pallas_call(
        spread_kernel,
        grid=(count // step,),
        in_specs=[
            pl.BlockSpec(memory_space=pltpu.SMEM),
            pl.BlockSpec((parts, step, grid, sticks), lambda i: (0, i, 0, 0)),
        ],
        out_specs=pl.BlockSpec((2, bands, grid, sticks), lambda i: (0, 0, 0, 0)),
        out_shape=jax.ShapeDtypeStruct((2, bands, grid, sticks), jnp.float32),
        cost_estimate=pl.CostEstimate(
            flops=4 * beta.size * bands, bytes_accessed=4 * beta.size, transcendentals=0
        ),
        name="back_project",
    )(coupled.reshape(-1), beta)


def per_device(groups, shards, psi, vloc, dv, beta, dij, atom_type, stick_xy, band_shift):
    _, bands, grid, own = psi.shape
    planes = vloc.shape[0]
    sticks = stick_xy.shape[0]
    radius = grid // 3
    side = 2 * radius
    atoms = atom_type.shape[0]
    per_atom = dij.shape[1]
    images = planes * bands

    cells = np.arange(grid)
    freqs = (np.arange(side) - radius) % grid
    z_inv = as_f32(np.stack(phases(cells, cells, grid, 1.0)))
    z_fwd = as_f32(np.stack(phases(cells, cells, grid, -1.0)))
    y_inv = as_f32(packed(phases(freqs, cells, grid, 1.0)).T)
    x_inv_re, x_inv_im = pad_part(*phases(freqs, cells, grid, 1.0), 1)
    x_inv = as_f32(packed((x_inv_re, x_inv_im)))
    x_fwd_re, x_fwd_im = pad_part(*phases(cells, freqs, grid, -1.0), 0)
    x_fwd = as_f32(packed((x_fwd_re, x_fwd_im)))
    y_fwd = as_f32(np.concatenate(phases(freqs, cells, grid, -1.0)))

    row_slot = frequency(stick_xy // grid, grid) + radius
    col_slot = frequency(stick_xy % grid, grid) + radius
    slot = row_slot * side + col_slot
    onehot = (slot[:, None] == jnp.arange(side * side, dtype=jnp.int32)[None, :]).astype(
        jnp.bfloat16
    )

    def widen(field):
        shaped = jnp.pad(field.reshape(planes, grid, grid), ((0, 0), (0, 0), (0, LANES - grid)))
        return jnp.concatenate([shaped, shaped], axis=2)[:, None]

    def to_real(coef):
        mixed = jnp.einsum("dkz,cbzs->dckbs", z_inv, coef, precision=high)
        lines = jnp.stack(
            [mixed[0, 0] - mixed[1, 1], mixed[0, 1] + mixed[1, 0]], axis=2
        ).reshape(shards, images * 2, own)
        got = lax.all_to_all(lines, "ga", split_axis=0, concat_axis=0)
        rows = jnp.moveaxis(got, 0, 1).reshape(images * 2, sticks)
        square = jnp.dot(hi_lo(rows), onehot, preferred_element_type=jnp.float32)
        square = (square[: images * 2] + square[images * 2 :]).reshape(images, 2 * side, side)
        along_y = jnp.einsum("ra,nak->nrk", y_inv, square, precision=high)
        joined = jnp.concatenate([along_y[:, :grid], along_y[:, grid:]], axis=2)
        field = jnp.einsum("nyk,kl->nyl", joined, x_inv, precision=high)
        return field.reshape(planes, bands, grid, 2 * LANES)

    def to_sticks(field):
        shaped = field.reshape(images, grid, 2 * LANES)
        along_x = jnp.einsum("nyl,lk->nyk", shaped, x_fwd, precision=high)
        mixed = jnp.einsum("ry,nyk->nrk", y_fwd, along_x, precision=high)
        square = jnp.stack(
            [
                mixed[:, :side, :side] - mixed[:, side:, side:],
                mixed[:, :side, side:] + mixed[:, side:, :side],
            ],
            axis=1,
        ).reshape(images * 2, side * side)
        rows = lax.dot_general(
            hi_lo(square), onehot, (((1,), (1,)), ((), ())), preferred_element_type=jnp.float32
        )
        rows = rows[: images * 2] + rows[images * 2 :]
        lines = jnp.moveaxis(rows.reshape(images * 2, shards, own), 1, 0)
        got = lax.all_to_all(lines, "ga", split_axis=0, concat_axis=0)
        got = got.reshape(grid, bands, 2, own)
        back = jnp.einsum("dkz,zbcs->dcbks", z_fwd, got, precision=high)
        return jnp.stack([back[0, 0] - back[1, 1], back[0, 1] + back[1, 0]])

    def total(pieces):
        flat = jnp.concatenate([piece.reshape(-1) for piece in pieces])
        summed = lax.psum(flat, "ga")
        done, at = [], 0
        for piece in pieces:
            done.append(summed[at : at + piece.size].reshape(piece.shape))
            at += piece.size
        return done

    def band_sum(values):
        return jnp.sum(values, axis=(0, 2, 3))

    def field_sum(values):
        return jnp.sum(values, axis=(0, 2, 3))

    start = lax.axis_index("ga") * own
    own_xy = lax.dynamic_slice_in_dim(stick_xy, start, own)
    freq_z = frequency(jnp.arange(grid, dtype=jnp.int32), grid)
    summed = (
        freq_z[:, None] ** 2
        + (frequency(own_xy // grid, grid) ** 2 + frequency(own_xy % grid, grid) ** 2)[None, :]
    )
    kinetic = summed.astype(jnp.float32) * (4.0 / (grid * grid))
    diagonal = (kinetic[None] + band_shift[:, None, None])[None]

    others = [
        lax.ppermute(psi, "band", [(src, (src + hop) % groups) for src in range(groups)])
        for hop in range(1, groups)
    ]
    gathered = jnp.concatenate([psi] + others, axis=1).astype(jnp.float32)

    vloc_wide = widen(vloc)
    psi_real = to_real(psi.astype(jnp.float32))
    image_dv = to_sticks(widen(dv) * psi_real)

    inv_norm = 1.0 / (2.0 * grid * sticks)
    inter_re = jnp.sum(gathered[:, :, None] * image_dv[:, None], axis=(0, 3, 4)) * inv_norm
    inter_im = (
        jnp.sum(
            gathered[0][:, None] * image_dv[1][None] - gathered[1][:, None] * image_dv[0][None],
            axis=(2, 3),
        )
        * inv_norm
    )
    inter_re, inter_im = total([inter_re, inter_im])
    wide_re = inter_re[:, :, None, None]
    wide_im = inter_im[:, :, None, None]
    psi_re, psi_im = gathered[0][:, None], gathered[1][:, None]
    rhs = (
        jnp.stack(
            [
                jnp.sum(wide_re * psi_re - wide_im * psi_im, axis=0),
                jnp.sum(wide_im * psi_re + wide_re * psi_im, axis=0),
            ]
        )
        - image_dv
    )

    kinds = jnp.arange(dij.shape[0], dtype=jnp.int32)
    onehot_type = (atom_type[:, None] == kinds[None, :]).astype(jnp.float32)
    selected = jnp.sum(onehot_type[:, :, None, None] * dij[None], axis=1)

    def couple(projected):
        shaped = projected.reshape(atoms, 1, per_atom, bands, 2)
        return jnp.sum(selected[:, :, :, None, None] * shaped, axis=2).reshape(projected.shape)

    field0 = to_real(rhs)
    local = to_sticks(vloc_wide * field0)
    proj0, norm0, curve0 = total(
        [
            project(beta, rhs),
            band_sum(rhs * rhs),
            band_sum(diagonal * rhs * rhs) + jnp.sum(vloc_wide * field0 * field0, axis=(0, 2, 3)),
        ]
    )
    coupled0 = couple(proj0)
    image = diagonal * rhs + local + back_project(beta, coupled0)
    alpha0 = norm0 / (curve0 + jnp.sum(proj0 * coupled0, axis=(0, 2)))
    residual = rhs - alpha0[None, :, None, None] * image

    field1 = to_real(residual)
    proj1, norm1, curve1, cross = total(
        [
            project(beta, residual),
            band_sum(residual * residual),
            band_sum(diagonal * residual * residual) + field_sum(vloc_wide * field1 * field1),
            band_sum(diagonal * residual * rhs) + field_sum(vloc_wide * field1 * field0),
        ]
    )
    ratio = norm1 / norm0
    proj1 = proj1 + ratio[None, :, None] * proj0
    curve1 = curve1 + 2.0 * ratio * cross + ratio * ratio * curve0
    alpha1 = norm1 / (curve1 + jnp.sum(proj1 * couple(proj1), axis=(0, 2)))
    keep = alpha0 + alpha1 * ratio
    response = keep[None, :, None, None] * rhs + alpha1[None, :, None, None] * residual

    real = psi_real * (
        keep[None, :, None, None] * field0 + alpha1[None, :, None, None] * field1
    )
    real = jnp.sum(real, axis=1)
    part = 4.0 * (real[:, :, :grid] + real[:, :, LANES : LANES + grid])
    part = jnp.moveaxis(part.reshape(planes, groups, grid // groups, grid), 1, 0)
    got = lax.all_to_all(part, "band", split_axis=0, concat_axis=0)
    density = jnp.sum(got, axis=0).reshape(planes, grid * grid // groups)
    return (response, density)


def solution(mesh):
    placed = (
        P(None, "band", None, "ga"),
        P("ga", None),
        P("ga", None),
        P(None, None, None, "ga"),
        P(),
        P(),
        P(),
        P("band"),
    )
    groups, shards = mesh.shape["band"], mesh.shape["ga"]

    def body(*args):
        return per_device(groups, shards, *args)

    return jax.shard_map(
        body,
        mesh=mesh,
        in_specs=placed,
        out_specs=(P(None, "band", None, "ga"), P("ga", "band")),
        check_vma=False,
    )
```

```python
import math

import jax
import jax.numpy as jnp
import numpy as np
from jax import lax
from jax.experimental import pallas as pl
from jax.experimental.pallas import tpu as pltpu
from jax.sharding import PartitionSpec as P

LANES = 128
high = lax.Precision.HIGH


def frequency(index, grid):
    return (index + grid // 2) % grid - grid // 2


def phases(rows, cols, grid, sign):
    angle = 2.0 * math.pi * ((rows[:, None] * cols[None, :]) % grid) / grid
    factor = 1.0 / math.sqrt(grid)
    return np.cos(angle) * factor, sign * np.sin(angle) * factor


def as_f32(table):
    return jnp.asarray(table.astype(np.float32))


def packed(table):
    real, imag = table
    return np.block([[real, imag], [-imag, real]])


def pad_part(real, imag, axis):
    width = LANES - real.shape[axis]
    pads = [(0, 0), (0, 0)]
    pads[axis] = (0, width)
    return np.pad(real, pads), np.pad(imag, pads)


def hi_lo(values):
    hi = lax.reduce_precision(values, 8, 7)
    return jnp.concatenate([hi, values - hi]).astype(jnp.bfloat16)


def project_kernel(beta_ref, vec_ref, out_ref):
    _, step, grid, lanes = beta_ref.shape
    bands = vec_ref.shape[1]
    some = math.gcd(step, 8)
    tile = 8

    def group(at, carry):
        first = at * some

        def body(t, sums):
            z = pl.ds(pl.multiple_of(t * tile, tile), tile)
            sums = list(sums)
            for lane in range(0, lanes, LANES):
                cut = pl.ds(lane, LANES)
                v_re = [vec_ref[0, b, z, cut] for b in range(bands)]
                v_im = [vec_ref[1, b, z, cut] for b in range(bands)]
                for j in range(some):
                    b_re = beta_ref[0, first + j, z, cut]
                    b_im = beta_ref[1, first + j, z, cut]
                    for b in range(bands):
                        to = (j * bands + b) * 2
                        sums[to] = sums[to] + (b_re * v_re[b] + b_im * v_im[b])
                        sums[to + 1] = sums[to + 1] + (b_re * v_im[b] - b_im * v_re[b])
            return tuple(sums)

        zero = jnp.zeros((tile, LANES), jnp.float32)
        sums = lax.fori_loop(0, grid // tile, body, (zero,) * (some * bands * 2))
        for j in range(some):
            mine = sums[j * bands * 2 : (j + 1) * bands * 2]
            out_ref[first + j] = jnp.concatenate(
                [jnp.sum(one, axis=0, keepdims=True) for one in mine], axis=0
            )
        return carry

    lax.fori_loop(0, step // some, group, 0)


def project(beta, vec):
    parts, count, grid, sticks = beta.shape
    bands = vec.shape[1]
    step = math.gcd(count, 16)
    out = pl.pallas_call(
        project_kernel,
        grid=(count // step,),
        in_specs=[
            pl.BlockSpec((parts, step, grid, sticks), lambda i: (0, i, 0, 0)),
            pl.BlockSpec(vec.shape, lambda i: (0, 0, 0, 0)),
        ],
        out_specs=pl.BlockSpec((step, 2 * bands, LANES), lambda i: (i, 0, 0)),
        out_shape=jax.ShapeDtypeStruct((count, 2 * bands, LANES), jnp.float32),
        cost_estimate=pl.CostEstimate(
            flops=4 * beta.size * bands, bytes_accessed=4 * beta.size, transcendentals=0
        ),
        name="project",
    )(beta, vec)
    return jnp.sum(out, axis=2).reshape(count, bands, 2)


def spread_kernel(coef_ref, beta_ref, out_ref):
    _, step, grid, lanes = beta_ref.shape
    bands = out_ref.shape[1]
    base = pl.program_id(0) * step
    rows = math.gcd(grid, 32)

    @pl.when(pl.program_id(0) == 0)
    def _():
        out_ref[...] = jnp.zeros_like(out_ref)

    def body(at, carry):
        z = pl.ds(pl.multiple_of(at * rows, rows), rows)
        re = [out_ref[0, b, z, :] for b in range(bands)]
        im = [out_ref[1, b, z, :] for b in range(bands)]
        for j in range(step):
            b_re = beta_ref[0, j, z, :]
            b_im = beta_ref[1, j, z, :]
            for b in range(bands):
                c_re = coef_ref[(base + j) * 2 * bands + 2 * b]
                c_im = coef_ref[(base + j) * 2 * bands + 2 * b + 1]
                re[b] = re[b] + (b_re * c_re - b_im * c_im)
                im[b] = im[b] + (b_re * c_im + b_im * c_re)
        for b in range(bands):
            out_ref[0, b, z, :] = re[b]
            out_ref[1, b, z, :] = im[b]
        return carry

    lax.fori_loop(0, grid // rows, body, 0)


def back_project(beta, coupled):
    parts, count, grid, sticks = beta.shape
    bands = coupled.shape[1]
    step = math.gcd(count, 16)
    return pl.pallas_call(
        spread_kernel,
        grid=(count // step,),
        in_specs=[
            pl.BlockSpec(memory_space=pltpu.SMEM),
            pl.BlockSpec((parts, step, grid, sticks), lambda i: (0, i, 0, 0)),
        ],
        out_specs=pl.BlockSpec((2, bands, grid, sticks), lambda i: (0, 0, 0, 0)),
        out_shape=jax.ShapeDtypeStruct((2, bands, grid, sticks), jnp.float32),
        cost_estimate=pl.CostEstimate(
            flops=4 * beta.size * bands, bytes_accessed=4 * beta.size, transcendentals=0
        ),
        name="back_project",
    )(coupled.reshape(-1), beta)


def push_kernel(axis, count, scatter, x_ref, out_ref, held, send_sem, recv_sem):
    me = lax.axis_index(axis)
    peers = [lax.rem(me + hop, count) for hop in range(1, count)]
    barrier = pltpu.get_barrier_semaphore()
    for peer in peers:
        pl.semaphore_signal(
            barrier, inc=1, device_id={axis: peer}, device_id_type=pl.DeviceIdType.MESH
        )
    held[me] = x_ref[me] if scatter else x_ref[...]
    pl.semaphore_wait(barrier, count - 1)
    copies = []
    for at, peer in enumerate(peers):
        copy = pltpu.make_async_remote_copy(
            src_ref=x_ref.at[peer] if scatter else x_ref,
            dst_ref=held.at[me],
            send_sem=send_sem.at[at],
            recv_sem=recv_sem.at[at],
            device_id={axis: peer},
            device_id_type=pl.DeviceIdType.MESH,
        )
        copy.start()
        copies.append(copy)
    for copy in copies:
        copy.wait()
    summed = held[0]
    for at in range(1, count):
        summed = summed + held[at]
    out_ref[...] = summed


def push_sum(x, axis, count, scatter, number):
    shape = x.shape[1:] if scatter else x.shape
    return pl.pallas_call(
        lambda *refs: push_kernel(axis, count, scatter, *refs),
        out_shape=jax.ShapeDtypeStruct(shape, x.dtype),
        in_specs=[pl.BlockSpec(memory_space=pltpu.VMEM)],
        out_specs=pl.BlockSpec(memory_space=pltpu.VMEM),
        scratch_shapes=[
            pltpu.VMEM((count,) + shape, x.dtype),
            pltpu.SemaphoreType.DMA((count - 1,)),
            pltpu.SemaphoreType.DMA((count - 1,)),
        ],
        compiler_params=pltpu.CompilerParams(collective_id=number, has_side_effects=True),
        name=f"push_sum_{number}",
    )(x)


def per_device(groups, shards, psi, vloc, dv, beta, dij, atom_type, stick_xy, band_shift):
    _, bands, grid, own = psi.shape
    planes = vloc.shape[0]
    sticks = stick_xy.shape[0]
    radius = grid // 3
    side = 2 * radius
    atoms = atom_type.shape[0]
    per_atom = dij.shape[1]
    images = planes * bands

    cells = np.arange(grid)
    freqs = (np.arange(side) - radius) % grid
    z_inv = as_f32(np.stack(phases(cells, cells, grid, 1.0)))
    z_fwd = as_f32(np.stack(phases(cells, cells, grid, -1.0)))
    y_inv = as_f32(packed(phases(freqs, cells, grid, 1.0)).T)
    x_inv_re, x_inv_im = pad_part(*phases(freqs, cells, grid, 1.0), 1)
    x_inv = as_f32(packed((x_inv_re, x_inv_im)))
    x_fwd_re, x_fwd_im = pad_part(*phases(cells, freqs, grid, -1.0), 0)
    x_fwd = as_f32(packed((x_fwd_re, x_fwd_im)))
    y_fwd = as_f32(np.concatenate(phases(freqs, cells, grid, -1.0)))

    row_slot = frequency(stick_xy // grid, grid) + radius
    col_slot = frequency(stick_xy % grid, grid) + radius
    slot = row_slot * side + col_slot
    onehot = (slot[:, None] == jnp.arange(side * side, dtype=jnp.int32)[None, :]).astype(
        jnp.bfloat16
    )

    def widen(field):
        shaped = jnp.pad(field.reshape(planes, grid, grid), ((0, 0), (0, 0), (0, LANES - grid)))
        return jnp.concatenate([shaped, shaped], axis=2)[:, None]

    def to_real(coef):
        mixed = jnp.einsum("dkz,cbzs->dckbs", z_inv, coef, precision=high)
        lines = jnp.stack(
            [mixed[0, 0] - mixed[1, 1], mixed[0, 1] + mixed[1, 0]], axis=2
        ).reshape(shards, images * 2, own)
        got = lax.all_to_all(lines, "ga", split_axis=0, concat_axis=0)
        rows = jnp.moveaxis(got, 0, 1).reshape(images * 2, sticks)
        square = jnp.dot(hi_lo(rows), onehot, preferred_element_type=jnp.float32)
        square = (square[: images * 2] + square[images * 2 :]).reshape(images, 2 * side, side)
        along_y = jnp.einsum("ra,nak->nrk", y_inv, square, precision=high)
        joined = jnp.concatenate([along_y[:, :grid], along_y[:, grid:]], axis=2)
        field = jnp.einsum("nyk,kl->nyl", joined, x_inv, precision=high)
        return field.reshape(planes, bands, grid, 2 * LANES)

    def to_sticks(field):
        shaped = field.reshape(images, grid, 2 * LANES)
        along_x = jnp.einsum("nyl,lk->nyk", shaped, x_fwd, precision=high)
        mixed = jnp.einsum("ry,nyk->nrk", y_fwd, along_x, precision=high)
        square = jnp.stack(
            [
                mixed[:, :side, :side] - mixed[:, side:, side:],
                mixed[:, :side, side:] + mixed[:, side:, :side],
            ],
            axis=1,
        ).reshape(images * 2, side * side)
        rows = lax.dot_general(
            hi_lo(square), onehot, (((1,), (1,)), ((), ())), preferred_element_type=jnp.float32
        )
        rows = rows[: images * 2] + rows[images * 2 :]
        lines = jnp.moveaxis(rows.reshape(images * 2, shards, own), 1, 0)
        got = lax.all_to_all(lines, "ga", split_axis=0, concat_axis=0)
        got = got.reshape(grid, bands, 2, own)
        back = jnp.einsum("dkz,zbcs->dcbks", z_fwd, got, precision=high)
        return jnp.stack([back[0, 0] - back[1, 1], back[0, 1] + back[1, 0]])

    def total(pieces, number):
        flat = jnp.concatenate([piece.reshape(-1) for piece in pieces])
        unit = 8 * LANES
        flat = jnp.pad(flat, (0, -flat.size % unit)).reshape(-1, LANES)
        summed = push_sum(flat, "ga", shards, False, number).reshape(-1)
        done, at = [], 0
        for piece in pieces:
            done.append(summed[at : at + piece.size].reshape(piece.shape))
            at += piece.size
        return done

    def band_sum(values):
        return jnp.sum(values, axis=(0, 2, 3))

    def field_sum(values):
        return jnp.sum(values, axis=(0, 2, 3))

    start = lax.axis_index("ga") * own
    own_xy = lax.dynamic_slice_in_dim(stick_xy, start, own)
    freq_z = frequency(jnp.arange(grid, dtype=jnp.int32), grid)
    summed = (
        freq_z[:, None] ** 2
        + (frequency(own_xy // grid, grid) ** 2 + frequency(own_xy % grid, grid) ** 2)[None, :]
    )
    kinetic = summed.astype(jnp.float32) * (4.0 / (grid * grid))
    diagonal = (kinetic[None] + band_shift[:, None, None])[None]

    others = [
        lax.ppermute(psi, "band", [(src, (src + hop) % groups) for src in range(groups)])
        for hop in range(1, groups)
    ]
    gathered = jnp.concatenate([psi] + others, axis=1).astype(jnp.float32)

    vloc_wide = widen(vloc)
    psi_real = to_real(psi.astype(jnp.float32))
    image_dv = to_sticks(widen(dv) * psi_real)

    inv_norm = 1.0 / (2.0 * grid * sticks)
    inter_re = jnp.sum(gathered[:, :, None] * image_dv[:, None], axis=(0, 3, 4)) * inv_norm
    inter_im = (
        jnp.sum(
            gathered[0][:, None] * image_dv[1][None] - gathered[1][:, None] * image_dv[0][None],
            axis=(2, 3),
        )
        * inv_norm
    )
    inter_re, inter_im = total([inter_re, inter_im], 0)
    wide_re = inter_re[:, :, None, None]
    wide_im = inter_im[:, :, None, None]
    psi_re, psi_im = gathered[0][:, None], gathered[1][:, None]
    rhs = (
        jnp.stack(
            [
                jnp.sum(wide_re * psi_re - wide_im * psi_im, axis=0),
                jnp.sum(wide_im * psi_re + wide_re * psi_im, axis=0),
            ]
        )
        - image_dv
    )

    kinds = jnp.arange(dij.shape[0], dtype=jnp.int32)
    onehot_type = (atom_type[:, None] == kinds[None, :]).astype(jnp.float32)
    selected = jnp.sum(onehot_type[:, :, None, None] * dij[None], axis=1)

    def couple(projected):
        shaped = projected.reshape(atoms, 1, per_atom, bands, 2)
        return jnp.sum(selected[:, :, :, None, None] * shaped, axis=2).reshape(projected.shape)

    field0 = to_real(rhs)
    local = to_sticks(vloc_wide * field0)
    proj0, norm0, curve0 = total(
        [
            project(beta, rhs),
            band_sum(rhs * rhs),
            band_sum(diagonal * rhs * rhs) + field_sum(vloc_wide * field0 * field0),
        ],
        1,
    )
    coupled0 = couple(proj0)
    image = diagonal * rhs + local + back_project(beta, coupled0)
    alpha0 = norm0 / (curve0 + jnp.sum(proj0 * coupled0, axis=(0, 2)))
    residual = rhs - alpha0[None, :, None, None] * image

    field1 = to_real(residual)
    proj1, norm1, curve1, cross = total(
        [
            project(beta, residual),
            band_sum(residual * residual),
            band_sum(diagonal * residual * residual) + field_sum(vloc_wide * field1 * field1),
            band_sum(diagonal * residual * rhs) + field_sum(vloc_wide * field1 * field0),
        ],
        2,
    )
    ratio = norm1 / norm0
    proj1 = proj1 + ratio[None, :, None] * proj0
    curve1 = curve1 + 2.0 * ratio * cross + ratio * ratio * curve0
    alpha1 = norm1 / (curve1 + jnp.sum(proj1 * couple(proj1), axis=(0, 2)))
    keep = alpha0 + alpha1 * ratio
    response = keep[None, :, None, None] * rhs + alpha1[None, :, None, None] * residual

    real = psi_real * (
        keep[None, :, None, None] * field0 + alpha1[None, :, None, None] * field1
    )
    real = jnp.sum(real, axis=1)
    part = 4.0 * (real[:, :, :grid] + real[:, :, LANES : LANES + grid])
    part = jnp.moveaxis(part.reshape(planes, groups, grid // groups, grid), 1, 0)
    density = push_sum(part, "band", groups, True, 3).reshape(planes, grid * grid // groups)
    return (response, density)


def solution(mesh):
    placed = (
        P(None, "band", None, "ga"),
        P("ga", None),
        P("ga", None),
        P(None, None, None, "ga"),
        P(),
        P(),
        P(),
        P("band"),
    )
    groups, shards = mesh.shape["band"], mesh.shape["ga"]

    def body(*args):
        return per_device(groups, shards, *args)

    return jax.shard_map(
        body,
        mesh=mesh,
        in_specs=placed,
        out_specs=(P(None, "band", None, "ga"), P("ga", "band")),
        check_vma=False,
    )
```

```python
import math

import jax
import jax.numpy as jnp
import numpy as np
from jax import lax
from jax.experimental import pallas as pl
from jax.experimental.pallas import tpu as pltpu
from jax.sharding import PartitionSpec as P

LANES = 128
STREAMS = 2
high = lax.Precision.HIGH


def frequency(index, grid):
    return (index + grid // 2) % grid - grid // 2


def phases(rows, cols, grid, sign):
    angle = 2.0 * math.pi * ((rows[:, None] * cols[None, :]) % grid) / grid
    factor = 1.0 / math.sqrt(grid)
    return np.cos(angle) * factor, sign * np.sin(angle) * factor


def as_f32(table):
    return jnp.asarray(table.astype(np.float32))


def packed(table):
    real, imag = table
    return np.block([[real, imag], [-imag, real]])


def pad_part(real, imag, axis):
    width = LANES - real.shape[axis]
    pads = [(0, 0), (0, 0)]
    pads[axis] = (0, width)
    return np.pad(real, pads), np.pad(imag, pads)


def hi_lo(values):
    hi = lax.reduce_precision(values, 8, 7)
    return jnp.concatenate([hi, values - hi]).astype(jnp.bfloat16)


def project_kernel(*refs):
    halves, vec_ref, out_ref = refs[:-2], refs[-2], refs[-1]
    _, some, grid, lanes = halves[0].shape
    bands = vec_ref.shape[1]
    tile = 8

    for at in range(len(halves) // 2):
        first = at * some
        re_ref, im_ref = halves[2 * at : 2 * at + 2]

        def body(t, sums, re_ref=re_ref, im_ref=im_ref):
            z = pl.ds(pl.multiple_of(t * tile, tile), tile)
            sums = list(sums)
            for lane in range(0, lanes, LANES):
                cut = pl.ds(lane, LANES)
                v_re = [vec_ref[0, b, z, cut] for b in range(bands)]
                v_im = [vec_ref[1, b, z, cut] for b in range(bands)]
                for j in range(some):
                    b_re = re_ref[0, j, z, cut]
                    b_im = im_ref[0, j, z, cut]
                    for b in range(bands):
                        to = (j * bands + b) * 2
                        sums[to] = sums[to] + (b_re * v_re[b] + b_im * v_im[b])
                        sums[to + 1] = sums[to + 1] + (b_re * v_im[b] - b_im * v_re[b])
            return tuple(sums)

        zero = jnp.zeros((tile, LANES), jnp.float32)
        sums = lax.fori_loop(0, grid // tile, body, (zero,) * (some * bands * 2))
        for j in range(some):
            mine = sums[j * bands * 2 : (j + 1) * bands * 2]
            out_ref[first + j] = jnp.concatenate(
                [jnp.sum(one, axis=0, keepdims=True) for one in mine], axis=0
            )


def beta_specs(parts, step, streams, grid, sticks):
    some = step // streams
    return [
        pl.BlockSpec((1, some, grid, sticks), lambda i, at=at, part=part: (part, streams * i + at, 0, 0))
        for at in range(streams)
        for part in range(parts)
    ]


def project(beta, vec):
    parts, count, grid, sticks = beta.shape
    bands = vec.shape[1]
    step = math.gcd(count, 16)
    out = pl.pallas_call(
        project_kernel,
        grid=(count // step,),
        in_specs=beta_specs(parts, step, STREAMS, grid, sticks)
        + [pl.BlockSpec(vec.shape, lambda i: (0, 0, 0, 0))],
        out_specs=pl.BlockSpec((step, 2 * bands, LANES), lambda i: (i, 0, 0)),
        out_shape=jax.ShapeDtypeStruct((count, 2 * bands, LANES), jnp.float32),
        cost_estimate=pl.CostEstimate(
            flops=4 * beta.size * bands, bytes_accessed=4 * beta.size, transcendentals=0
        ),
        name="project",
    )(*[beta] * (parts * STREAMS), vec)
    return jnp.sum(out, axis=2).reshape(count, bands, 2)


def spread_kernel(*refs):
    coef_ref, halves, out_ref = refs[0], refs[1:-1], refs[-1]
    _, some, grid, lanes = halves[0].shape
    step = some * (len(halves) // 2)
    bands = out_ref.shape[1]
    base = pl.program_id(0) * step
    rows = math.gcd(grid, 32)

    @pl.when(pl.program_id(0) == 0)
    def _():
        out_ref[...] = jnp.zeros_like(out_ref)

    def body(at, carry):
        z = pl.ds(pl.multiple_of(at * rows, rows), rows)
        re = [out_ref[0, b, z, :] for b in range(bands)]
        im = [out_ref[1, b, z, :] for b in range(bands)]
        for j in range(step):
            b_re = halves[j // some * 2][0, j % some, z, :]
            b_im = halves[j // some * 2 + 1][0, j % some, z, :]
            for b in range(bands):
                c_re = coef_ref[(base + j) * 2 * bands + 2 * b]
                c_im = coef_ref[(base + j) * 2 * bands + 2 * b + 1]
                re[b] = re[b] + (b_re * c_re - b_im * c_im)
                im[b] = im[b] + (b_re * c_im + b_im * c_re)
        for b in range(bands):
            out_ref[0, b, z, :] = re[b]
            out_ref[1, b, z, :] = im[b]
        return carry

    lax.fori_loop(0, grid // rows, body, 0)


def back_project(beta, coupled):
    parts, count, grid, sticks = beta.shape
    bands = coupled.shape[1]
    step = math.gcd(count, 16)
    return pl.pallas_call(
        spread_kernel,
        grid=(count // step,),
        in_specs=[pl.BlockSpec(memory_space=pltpu.SMEM)]
        + beta_specs(parts, step, STREAMS, grid, sticks),
        out_specs=pl.BlockSpec((2, bands, grid, sticks), lambda i: (0, 0, 0, 0)),
        out_shape=jax.ShapeDtypeStruct((2, bands, grid, sticks), jnp.float32),
        cost_estimate=pl.CostEstimate(
            flops=4 * beta.size * bands, bytes_accessed=4 * beta.size, transcendentals=0
        ),
        name="back_project",
    )(coupled.reshape(-1), *[beta] * (parts * STREAMS))


def push_kernel(axis, count, scatter, x_ref, out_ref, held, send_sem, recv_sem):
    me = lax.axis_index(axis)
    peers = [lax.rem(me + hop, count) for hop in range(1, count)]
    barrier = pltpu.get_barrier_semaphore()
    for peer in peers:
        pl.semaphore_signal(
            barrier, inc=1, device_id={axis: peer}, device_id_type=pl.DeviceIdType.MESH
        )
    held[me] = x_ref[me] if scatter else x_ref[...]
    pl.semaphore_wait(barrier, count - 1)
    copies = []
    for at, peer in enumerate(peers):
        copy = pltpu.make_async_remote_copy(
            src_ref=x_ref.at[peer] if scatter else x_ref,
            dst_ref=held.at[me],
            send_sem=send_sem.at[at],
            recv_sem=recv_sem.at[at],
            device_id={axis: peer},
            device_id_type=pl.DeviceIdType.MESH,
        )
        copy.start()
        copies.append(copy)
    for copy in copies:
        copy.wait()
    summed = held[0]
    for at in range(1, count):
        summed = summed + held[at]
    out_ref[...] = summed


def push_sum(x, axis, count, scatter, number):
    shape = x.shape[1:] if scatter else x.shape
    return pl.pallas_call(
        lambda *refs: push_kernel(axis, count, scatter, *refs),
        out_shape=jax.ShapeDtypeStruct(shape, x.dtype),
        in_specs=[pl.BlockSpec(memory_space=pltpu.VMEM)],
        out_specs=pl.BlockSpec(memory_space=pltpu.VMEM),
        scratch_shapes=[
            pltpu.VMEM((count,) + shape, x.dtype),
            pltpu.SemaphoreType.DMA((count - 1,)),
            pltpu.SemaphoreType.DMA((count - 1,)),
        ],
        compiler_params=pltpu.CompilerParams(collective_id=number, has_side_effects=True),
        name=f"push_sum_{number}",
    )(x)


def per_device(groups, shards, psi, vloc, dv, beta, dij, atom_type, stick_xy, band_shift):
    _, bands, grid, own = psi.shape
    planes = vloc.shape[0]
    sticks = stick_xy.shape[0]
    radius = grid // 3
    side = 2 * radius
    atoms = atom_type.shape[0]
    per_atom = dij.shape[1]
    images = planes * bands

    cells = np.arange(grid)
    freqs = (np.arange(side) - radius) % grid
    z_inv = as_f32(np.stack(phases(cells, cells, grid, 1.0)))
    z_fwd = as_f32(np.stack(phases(cells, cells, grid, -1.0)))
    y_inv = as_f32(packed(phases(freqs, cells, grid, 1.0)).T)
    x_inv_re, x_inv_im = pad_part(*phases(freqs, cells, grid, 1.0), 1)
    x_inv = as_f32(packed((x_inv_re, x_inv_im)))
    x_fwd_re, x_fwd_im = pad_part(*phases(cells, freqs, grid, -1.0), 0)
    x_fwd = as_f32(packed((x_fwd_re, x_fwd_im)))
    y_fwd = as_f32(np.concatenate(phases(freqs, cells, grid, -1.0)))

    row_slot = frequency(stick_xy // grid, grid) + radius
    col_slot = frequency(stick_xy % grid, grid) + radius
    slot = row_slot * side + col_slot
    onehot = (slot[:, None] == jnp.arange(side * side, dtype=jnp.int32)[None, :]).astype(
        jnp.bfloat16
    )

    def widen(field):
        shaped = jnp.pad(field.reshape(planes, grid, grid), ((0, 0), (0, 0), (0, LANES - grid)))
        return jnp.concatenate([shaped, shaped], axis=2)[:, None]

    def to_real(coef):
        mixed = jnp.einsum("dkz,cbzs->dckbs", z_inv, coef, precision=high)
        lines = jnp.stack(
            [mixed[0, 0] - mixed[1, 1], mixed[0, 1] + mixed[1, 0]], axis=2
        ).reshape(shards, images * 2, own)
        got = lax.all_to_all(lines, "ga", split_axis=0, concat_axis=0)
        rows = jnp.moveaxis(got, 0, 1).reshape(images * 2, sticks)
        square = jnp.dot(hi_lo(rows), onehot, preferred_element_type=jnp.float32)
        square = (square[: images * 2] + square[images * 2 :]).reshape(images, 2 * side, side)
        along_y = jnp.einsum("ra,nak->nrk", y_inv, square, precision=high)
        joined = jnp.concatenate([along_y[:, :grid], along_y[:, grid:]], axis=2)
        field = jnp.einsum("nyk,kl->nyl", joined, x_inv, precision=high)
        return field.reshape(planes, bands, grid, 2 * LANES)

    def to_sticks(field):
        shaped = field.reshape(images, grid, 2 * LANES)
        along_x = jnp.einsum("nyl,lk->nyk", shaped, x_fwd, precision=high)
        mixed = jnp.einsum("ry,nyk->nrk", y_fwd, along_x, precision=high)
        square = jnp.stack(
            [
                mixed[:, :side, :side] - mixed[:, side:, side:],
                mixed[:, :side, side:] + mixed[:, side:, :side],
            ],
            axis=1,
        ).reshape(images * 2, side * side)
        rows = lax.dot_general(
            hi_lo(square), onehot, (((1,), (1,)), ((), ())), preferred_element_type=jnp.float32
        )
        rows = rows[: images * 2] + rows[images * 2 :]
        lines = jnp.moveaxis(rows.reshape(images * 2, shards, own), 1, 0)
        got = lax.all_to_all(lines, "ga", split_axis=0, concat_axis=0)
        got = got.reshape(grid, bands, 2, own)
        back = jnp.einsum("dkz,zbcs->dcbks", z_fwd, got, precision=high)
        return jnp.stack([back[0, 0] - back[1, 1], back[0, 1] + back[1, 0]])

    def total(pieces, number):
        flat = jnp.concatenate([piece.reshape(-1) for piece in pieces])
        unit = 8 * LANES
        flat = jnp.pad(flat, (0, -flat.size % unit)).reshape(-1, LANES)
        summed = push_sum(flat, "ga", shards, False, number).reshape(-1)
        done, at = [], 0
        for piece in pieces:
            done.append(summed[at : at + piece.size].reshape(piece.shape))
            at += piece.size
        return done

    def band_sum(values):
        return jnp.sum(values, axis=(0, 2, 3))

    def field_sum(values):
        return jnp.sum(values, axis=(0, 2, 3))

    start = lax.axis_index("ga") * own
    own_xy = lax.dynamic_slice_in_dim(stick_xy, start, own)
    freq_z = frequency(jnp.arange(grid, dtype=jnp.int32), grid)
    summed = (
        freq_z[:, None] ** 2
        + (frequency(own_xy // grid, grid) ** 2 + frequency(own_xy % grid, grid) ** 2)[None, :]
    )
    kinetic = summed.astype(jnp.float32) * (4.0 / (grid * grid))
    diagonal = (kinetic[None] + band_shift[:, None, None])[None]

    others = [
        lax.ppermute(psi, "band", [(src, (src + hop) % groups) for src in range(groups)])
        for hop in range(1, groups)
    ]
    gathered = jnp.concatenate([psi] + others, axis=1).astype(jnp.float32)

    vloc_wide = widen(vloc)
    psi_real = to_real(psi.astype(jnp.float32))
    image_dv = to_sticks(widen(dv) * psi_real)

    inv_norm = 1.0 / (2.0 * grid * sticks)
    inter_re = jnp.sum(gathered[:, :, None] * image_dv[:, None], axis=(0, 3, 4)) * inv_norm
    inter_im = (
        jnp.sum(
            gathered[0][:, None] * image_dv[1][None] - gathered[1][:, None] * image_dv[0][None],
            axis=(2, 3),
        )
        * inv_norm
    )
    inter_re, inter_im = total([inter_re, inter_im], 0)
    wide_re = inter_re[:, :, None, None]
    wide_im = inter_im[:, :, None, None]
    psi_re, psi_im = gathered[0][:, None], gathered[1][:, None]
    rhs = (
        jnp.stack(
            [
                jnp.sum(wide_re * psi_re - wide_im * psi_im, axis=0),
                jnp.sum(wide_im * psi_re + wide_re * psi_im, axis=0),
            ]
        )
        - image_dv
    )

    kinds = jnp.arange(dij.shape[0], dtype=jnp.int32)
    onehot_type = (atom_type[:, None] == kinds[None, :]).astype(jnp.float32)
    selected = jnp.sum(onehot_type[:, :, None, None] * dij[None], axis=1)

    def couple(projected):
        shaped = projected.reshape(atoms, 1, per_atom, bands, 2)
        return jnp.sum(selected[:, :, :, None, None] * shaped, axis=2).reshape(projected.shape)

    field0 = to_real(rhs)
    local = to_sticks(vloc_wide * field0)
    proj0, norm0, curve0 = total(
        [
            project(beta, rhs),
            band_sum(rhs * rhs),
            band_sum(diagonal * rhs * rhs) + field_sum(vloc_wide * field0 * field0),
        ],
        1,
    )
    coupled0 = couple(proj0)
    image = diagonal * rhs + local + back_project(beta, coupled0)
    alpha0 = norm0 / (curve0 + jnp.sum(proj0 * coupled0, axis=(0, 2)))
    residual = rhs - alpha0[None, :, None, None] * image

    field1 = to_real(residual)
    proj1, norm1, curve1, cross = total(
        [
            project(beta, residual),
            band_sum(residual * residual),
            band_sum(diagonal * residual * residual) + field_sum(vloc_wide * field1 * field1),
            band_sum(diagonal * residual * rhs) + field_sum(vloc_wide * field1 * field0),
        ],
        2,
    )
    ratio = norm1 / norm0
    proj1 = proj1 + ratio[None, :, None] * proj0
    curve1 = curve1 + 2.0 * ratio * cross + ratio * ratio * curve0
    alpha1 = norm1 / (curve1 + jnp.sum(proj1 * couple(proj1), axis=(0, 2)))
    keep = alpha0 + alpha1 * ratio
    response = keep[None, :, None, None] * rhs + alpha1[None, :, None, None] * residual

    real = psi_real * (
        keep[None, :, None, None] * field0 + alpha1[None, :, None, None] * field1
    )
    real = jnp.sum(real, axis=1)
    part = 4.0 * (real[:, :, :grid] + real[:, :, LANES : LANES + grid])
    part = jnp.moveaxis(part.reshape(planes, groups, grid // groups, grid), 1, 0)
    if part[0].size % LANES == 0:
        part = part.reshape(groups, -1, LANES)
    density = push_sum(part, "band", groups, True, 3).reshape(planes, grid * grid // groups)
    return (response, density)


def solution(mesh):
    placed = (
        P(None, "band", None, "ga"),
        P("ga", None),
        P("ga", None),
        P(None, None, None, "ga"),
        P(),
        P(),
        P(),
        P("band"),
    )
    groups, shards = mesh.shape["band"], mesh.shape["ga"]

    def body(*args):
        return per_device(groups, shards, *args)

    return jax.shard_map(
        body,
        mesh=mesh,
        in_specs=placed,
        out_specs=(P(None, "band", None, "ga"), P("ga", "band")),
        check_vma=False,
    )
```

```python
import math

import jax
import jax.numpy as jnp
import numpy as np
from jax import lax
from jax.experimental import pallas as pl
from jax.experimental.pallas import tpu as pltpu
from jax.sharding import PartitionSpec as P

LANES = 128
STREAMS = 4
high = lax.Precision.HIGH


def frequency(index, grid):
    return (index + grid // 2) % grid - grid // 2


def phases(rows, cols, grid, sign):
    angle = 2.0 * math.pi * ((rows[:, None] * cols[None, :]) % grid) / grid
    factor = 1.0 / math.sqrt(grid)
    return np.cos(angle) * factor, sign * np.sin(angle) * factor


def as_f32(table):
    return jnp.asarray(table.astype(np.float32))


def packed(table):
    real, imag = table
    return np.block([[real, imag], [-imag, real]])


def pad_part(real, imag, axis):
    width = LANES - real.shape[axis]
    pads = [(0, 0), (0, 0)]
    pads[axis] = (0, width)
    return np.pad(real, pads), np.pad(imag, pads)


def hi_lo(values):
    hi = lax.reduce_precision(values, 8, 7)
    return jnp.concatenate([hi, values - hi]).astype(jnp.bfloat16)


def project_kernel(*refs):
    halves, vec_ref, out_ref = refs[:-2], refs[-2], refs[-1]
    _, some, grid, lanes = halves[0].shape
    bands = vec_ref.shape[1]
    tile = 8

    for at in range(len(halves) // 2):
        first = at * some
        re_ref, im_ref = halves[2 * at : 2 * at + 2]

        def body(t, sums, re_ref=re_ref, im_ref=im_ref):
            z = pl.ds(pl.multiple_of(t * tile, tile), tile)
            sums = list(sums)
            for lane in range(0, lanes, LANES):
                cut = pl.ds(lane, LANES)
                v_re = [vec_ref[0, b, z, cut] for b in range(bands)]
                v_im = [vec_ref[1, b, z, cut] for b in range(bands)]
                for j in range(some):
                    b_re = re_ref[0, j, z, cut]
                    b_im = im_ref[0, j, z, cut]
                    for b in range(bands):
                        to = (j * bands + b) * 2
                        sums[to] = sums[to] + (b_re * v_re[b] + b_im * v_im[b])
                        sums[to + 1] = sums[to + 1] + (b_re * v_im[b] - b_im * v_re[b])
            return tuple(sums)

        zero = jnp.zeros((tile, LANES), jnp.float32)
        sums = lax.fori_loop(0, grid // tile, body, (zero,) * (some * bands * 2))
        for j in range(some):
            mine = sums[j * bands * 2 : (j + 1) * bands * 2]
            out_ref[first + j] = jnp.concatenate(
                [jnp.sum(one, axis=0, keepdims=True) for one in mine], axis=0
            )


def beta_specs(parts, step, streams, grid, sticks):
    some = step // streams
    return [
        pl.BlockSpec((1, some, grid, sticks), lambda i, at=at, part=part: (part, streams * i + at, 0, 0))
        for at in range(streams)
        for part in range(parts)
    ]


def project(beta, vec):
    parts, count, grid, sticks = beta.shape
    bands = vec.shape[1]
    step = math.gcd(count, 32)
    out = pl.pallas_call(
        project_kernel,
        grid=(count // step,),
        in_specs=beta_specs(parts, step, STREAMS, grid, sticks)
        + [pl.BlockSpec(vec.shape, lambda i: (0, 0, 0, 0))],
        out_specs=pl.BlockSpec((step, 2 * bands, LANES), lambda i: (i, 0, 0)),
        out_shape=jax.ShapeDtypeStruct((count, 2 * bands, LANES), jnp.float32),
        cost_estimate=pl.CostEstimate(
            flops=4 * beta.size * bands, bytes_accessed=4 * beta.size, transcendentals=0
        ),
        name="project",
    )(*[beta] * (parts * STREAMS), vec)
    return jnp.sum(out, axis=2).reshape(count, bands, 2)


def spread_kernel(*refs):
    coef_ref, halves, out_ref = refs[0], refs[1:-1], refs[-1]
    _, some, grid, lanes = halves[0].shape
    step = some * (len(halves) // 2)
    bands = out_ref.shape[1]
    base = pl.program_id(0) * step
    rows = math.gcd(grid, 32)

    @pl.when(pl.program_id(0) == 0)
    def _():
        out_ref[...] = jnp.zeros_like(out_ref)

    def body(at, carry):
        z = pl.ds(pl.multiple_of(at * rows, rows), rows)
        re = [out_ref[0, b, z, :] for b in range(bands)]
        im = [out_ref[1, b, z, :] for b in range(bands)]
        for j in range(step):
            b_re = halves[j // some * 2][0, j % some, z, :]
            b_im = halves[j // some * 2 + 1][0, j % some, z, :]
            for b in range(bands):
                c_re = coef_ref[(base + j) * 2 * bands + 2 * b]
                c_im = coef_ref[(base + j) * 2 * bands + 2 * b + 1]
                re[b] = re[b] + (b_re * c_re - b_im * c_im)
                im[b] = im[b] + (b_re * c_im + b_im * c_re)
        for b in range(bands):
            out_ref[0, b, z, :] = re[b]
            out_ref[1, b, z, :] = im[b]
        return carry

    lax.fori_loop(0, grid // rows, body, 0)


def back_project(beta, coupled):
    parts, count, grid, sticks = beta.shape
    bands = coupled.shape[1]
    step = math.gcd(count, 32)
    return pl.pallas_call(
        spread_kernel,
        grid=(count // step,),
        in_specs=[pl.BlockSpec(memory_space=pltpu.SMEM)]
        + beta_specs(parts, step, STREAMS, grid, sticks),
        out_specs=pl.BlockSpec((2, bands, grid, sticks), lambda i: (0, 0, 0, 0)),
        out_shape=jax.ShapeDtypeStruct((2, bands, grid, sticks), jnp.float32),
        cost_estimate=pl.CostEstimate(
            flops=4 * beta.size * bands, bytes_accessed=4 * beta.size, transcendentals=0
        ),
        name="back_project",
    )(coupled.reshape(-1), *[beta] * (parts * STREAMS))


def push_kernel(axis, count, scatter, x_ref, out_ref, held, send_sem, recv_sem):
    me = lax.axis_index(axis)
    peers = [lax.rem(me + hop, count) for hop in range(1, count)]
    barrier = pltpu.get_barrier_semaphore()
    for peer in peers:
        pl.semaphore_signal(
            barrier, inc=1, device_id={axis: peer}, device_id_type=pl.DeviceIdType.MESH
        )
    held[me] = x_ref[me] if scatter else x_ref[...]
    pl.semaphore_wait(barrier, count - 1)
    copies = []
    for at, peer in enumerate(peers):
        copy = pltpu.make_async_remote_copy(
            src_ref=x_ref.at[peer] if scatter else x_ref,
            dst_ref=held.at[me],
            send_sem=send_sem.at[at],
            recv_sem=recv_sem.at[at],
            device_id={axis: peer},
            device_id_type=pl.DeviceIdType.MESH,
        )
        copy.start()
        copies.append(copy)
    for copy in copies:
        copy.wait()
    summed = held[0]
    for at in range(1, count):
        summed = summed + held[at]
    out_ref[...] = summed


def push_sum(x, axis, count, scatter, number):
    shape = x.shape[1:] if scatter else x.shape
    return pl.pallas_call(
        lambda *refs: push_kernel(axis, count, scatter, *refs),
        out_shape=jax.ShapeDtypeStruct(shape, x.dtype),
        in_specs=[pl.BlockSpec(memory_space=pltpu.VMEM)],
        out_specs=pl.BlockSpec(memory_space=pltpu.VMEM),
        scratch_shapes=[
            pltpu.VMEM((count,) + shape, x.dtype),
            pltpu.SemaphoreType.DMA((count - 1,)),
            pltpu.SemaphoreType.DMA((count - 1,)),
        ],
        compiler_params=pltpu.CompilerParams(collective_id=number, has_side_effects=True),
        name=f"push_sum_{number}",
    )(x)


def per_device(groups, shards, psi, vloc, dv, beta, dij, atom_type, stick_xy, band_shift):
    _, bands, grid, own = psi.shape
    planes = vloc.shape[0]
    sticks = stick_xy.shape[0]
    radius = grid // 3
    side = 2 * radius
    atoms = atom_type.shape[0]
    per_atom = dij.shape[1]
    images = planes * bands

    cells = np.arange(grid)
    freqs = (np.arange(side) - radius) % grid
    z_inv = as_f32(np.stack(phases(cells, cells, grid, 1.0)))
    z_fwd = as_f32(np.stack(phases(cells, cells, grid, -1.0)))
    y_inv = as_f32(packed(phases(freqs, cells, grid, 1.0)).T)
    x_inv_re, x_inv_im = pad_part(*phases(freqs, cells, grid, 1.0), 1)
    x_inv = as_f32(packed((x_inv_re, x_inv_im)))
    x_fwd_re, x_fwd_im = pad_part(*phases(cells, freqs, grid, -1.0), 0)
    x_fwd = as_f32(packed((x_fwd_re, x_fwd_im)))
    y_fwd = as_f32(np.concatenate(phases(freqs, cells, grid, -1.0)))

    row_slot = frequency(stick_xy // grid, grid) + radius
    col_slot = frequency(stick_xy % grid, grid) + radius
    slot = row_slot * side + col_slot
    onehot = (slot[:, None] == jnp.arange(side * side, dtype=jnp.int32)[None, :]).astype(
        jnp.bfloat16
    )

    def widen(field):
        shaped = jnp.pad(field.reshape(planes, grid, grid), ((0, 0), (0, 0), (0, LANES - grid)))
        return jnp.concatenate([shaped, shaped], axis=2)[:, None]

    def to_real(coef):
        mixed = jnp.einsum("dkz,cbzs->dckbs", z_inv, coef, precision=high)
        lines = jnp.stack(
            [mixed[0, 0] - mixed[1, 1], mixed[0, 1] + mixed[1, 0]], axis=2
        ).reshape(shards, images * 2, own)
        got = lax.all_to_all(lines, "ga", split_axis=0, concat_axis=0)
        rows = jnp.moveaxis(got, 0, 1).reshape(images * 2, sticks)
        square = jnp.dot(hi_lo(rows), onehot, preferred_element_type=jnp.float32)
        square = (square[: images * 2] + square[images * 2 :]).reshape(images, 2 * side, side)
        along_y = jnp.einsum("ra,nak->nrk", y_inv, square, precision=high)
        joined = jnp.concatenate([along_y[:, :grid], along_y[:, grid:]], axis=2)
        field = jnp.einsum("nyk,kl->nyl", joined, x_inv, precision=high)
        return field.reshape(planes, bands, grid, 2 * LANES)

    def to_sticks(field):
        shaped = field.reshape(images, grid, 2 * LANES)
        along_x = jnp.einsum("nyl,lk->nyk", shaped, x_fwd, precision=high)
        mixed = jnp.einsum("ry,nyk->nrk", y_fwd, along_x, precision=high)
        square = jnp.stack(
            [
                mixed[:, :side, :side] - mixed[:, side:, side:],
                mixed[:, :side, side:] + mixed[:, side:, :side],
            ],
            axis=1,
        ).reshape(images * 2, side * side)
        rows = lax.dot_general(
            hi_lo(square), onehot, (((1,), (1,)), ((), ())), preferred_element_type=jnp.float32
        )
        rows = rows[: images * 2] + rows[images * 2 :]
        lines = jnp.moveaxis(rows.reshape(images * 2, shards, own), 1, 0)
        got = lax.all_to_all(lines, "ga", split_axis=0, concat_axis=0)
        got = got.reshape(grid, bands, 2, own)
        back = jnp.einsum("dkz,zbcs->dcbks", z_fwd, got, precision=high)
        return jnp.stack([back[0, 0] - back[1, 1], back[0, 1] + back[1, 0]])

    def total(pieces, number):
        flat = jnp.concatenate([piece.reshape(-1) for piece in pieces])
        unit = 8 * LANES
        flat = jnp.pad(flat, (0, -flat.size % unit)).reshape(-1, LANES)
        summed = push_sum(flat, "ga", shards, False, number).reshape(-1)
        done, at = [], 0
        for piece in pieces:
            done.append(summed[at : at + piece.size].reshape(piece.shape))
            at += piece.size
        return done

    def band_sum(values):
        return jnp.sum(values, axis=(0, 2, 3))

    def field_sum(values):
        return jnp.sum(values, axis=(0, 2, 3))

    start = lax.axis_index("ga") * own
    own_xy = lax.dynamic_slice_in_dim(stick_xy, start, own)
    freq_z = frequency(jnp.arange(grid, dtype=jnp.int32), grid)
    summed = (
        freq_z[:, None] ** 2
        + (frequency(own_xy // grid, grid) ** 2 + frequency(own_xy % grid, grid) ** 2)[None, :]
    )
    kinetic = summed.astype(jnp.float32) * (4.0 / (grid * grid))
    diagonal = (kinetic[None] + band_shift[:, None, None])[None]

    others = [
        lax.ppermute(psi, "band", [(src, (src + hop) % groups) for src in range(groups)])
        for hop in range(1, groups)
    ]
    gathered = jnp.concatenate([psi] + others, axis=1).astype(jnp.float32)

    vloc_wide = widen(vloc)
    psi_real = to_real(psi.astype(jnp.float32))
    image_dv = to_sticks(widen(dv) * psi_real)

    inv_norm = 1.0 / (2.0 * grid * sticks)
    inter_re = jnp.sum(gathered[:, :, None] * image_dv[:, None], axis=(0, 3, 4)) * inv_norm
    inter_im = (
        jnp.sum(
            gathered[0][:, None] * image_dv[1][None] - gathered[1][:, None] * image_dv[0][None],
            axis=(2, 3),
        )
        * inv_norm
    )
    inter_re, inter_im = total([inter_re, inter_im], 0)
    wide_re = inter_re[:, :, None, None]
    wide_im = inter_im[:, :, None, None]
    psi_re, psi_im = gathered[0][:, None], gathered[1][:, None]
    rhs = (
        jnp.stack(
            [
                jnp.sum(wide_re * psi_re - wide_im * psi_im, axis=0),
                jnp.sum(wide_im * psi_re + wide_re * psi_im, axis=0),
            ]
        )
        - image_dv
    )

    kinds = jnp.arange(dij.shape[0], dtype=jnp.int32)
    onehot_type = (atom_type[:, None] == kinds[None, :]).astype(jnp.float32)
    selected = jnp.sum(onehot_type[:, :, None, None] * dij[None], axis=1)

    def couple(projected):
        shaped = projected.reshape(atoms, 1, per_atom, bands, 2)
        return jnp.sum(selected[:, :, :, None, None] * shaped, axis=2).reshape(projected.shape)

    field0 = to_real(rhs)
    local = to_sticks(vloc_wide * field0)
    proj0, norm0, curve0 = total(
        [
            project(beta, rhs),
            band_sum(rhs * rhs),
            band_sum(diagonal * rhs * rhs) + field_sum(vloc_wide * field0 * field0),
        ],
        1,
    )
    coupled0 = couple(proj0)
    image = diagonal * rhs + local + back_project(beta, coupled0)
    alpha0 = norm0 / (curve0 + jnp.sum(proj0 * coupled0, axis=(0, 2)))
    residual = rhs - alpha0[None, :, None, None] * image

    field1 = to_real(residual)
    proj1, norm1, curve1, cross = total(
        [
            project(beta, residual),
            band_sum(residual * residual),
            band_sum(diagonal * residual * residual) + field_sum(vloc_wide * field1 * field1),
            band_sum(diagonal * residual * rhs) + field_sum(vloc_wide * field1 * field0),
        ],
        2,
    )
    ratio = norm1 / norm0
    proj1 = proj1 + ratio[None, :, None] * proj0
    curve1 = curve1 + 2.0 * ratio * cross + ratio * ratio * curve0
    alpha1 = norm1 / (curve1 + jnp.sum(proj1 * couple(proj1), axis=(0, 2)))
    keep = alpha0 + alpha1 * ratio
    response = keep[None, :, None, None] * rhs + alpha1[None, :, None, None] * residual

    real = psi_real * (
        keep[None, :, None, None] * field0 + alpha1[None, :, None, None] * field1
    )
    real = jnp.sum(real, axis=1)
    part = 4.0 * (real[:, :, :grid] + real[:, :, LANES : LANES + grid])
    part = jnp.moveaxis(part.reshape(planes, groups, grid // groups, grid), 1, 0)
    if part[0].size % LANES == 0:
        part = part.reshape(groups, -1, LANES)
    density = push_sum(part, "band", groups, True, 3).reshape(planes, grid * grid // groups)
    return (response, density)


def solution(mesh):
    placed = (
        P(None, "band", None, "ga"),
        P("ga", None),
        P("ga", None),
        P(None, None, None, "ga"),
        P(),
        P(),
        P(),
        P("band"),
    )
    groups, shards = mesh.shape["band"], mesh.shape["ga"]

    def body(*args):
        return per_device(groups, shards, *args)

    return jax.shard_map(
        body,
        mesh=mesh,
        in_specs=placed,
        out_specs=(P(None, "band", None, "ga"), P("ga", "band")),
        check_vma=False,
    )
```
